32 devices in a mesh: section: 4 (over y, core), outer: 2 (over x), inner: 4 (over z).
Axes of the slice: x: 2, y: 2, z: 4, core: 2. Of those that a mesh axis runs over, the one named last changes fastest.
Arguments:
- projected: bfloat16 [4, 1024, 1280], P('section', ('outer', 'inner')), may hold values from -64 to 64
- positions: int32 [1024], replicated, may hold values from 0 to 1023, as said below
- out_weight: bfloat16 [4, 1024, 16384], P('section', None, ('outer', 'inner')), may hold values from -1.5 to 1.5
- residual: bfloat16 [4, 1024, 16384], P('section', None, ('outer', 'inner')), may hold values from -8 to 8
- norm_gain: bfloat16 [4, 16384], P('section', ('outer', 'inner')), may hold values from 0.099609375 to 1.8984375
- next_weight: bfloat16 [4, 16384, 1280], P('section', ('outer', 'inner')), may hold values from -0.046875 to 0.046875
Outputs:
- next_projected: bfloat16 [4, 1024, 1280], P('section', ('outer', 'inner'))
- stream: bfloat16 [4, 1024, 16384], P('section', None, ('outer', 'inner'))
The draws below stay inside these ranges and needn't reach their ends.
Inputs may be any that keep to these rules, and one draw needn't show every extreme that they name: Each aligned run of 64 stored tokens holds consecutive positions starting at a multiple of 64; every position 0 to 1023 is stored once.
All inputs are finite; a program needn't handle non-finite values.
Results may differ from the reference program's by a relative error of at most 0.023.
Values may be sent and summed in bfloat16 or wider, within the bound.
A program may use at most 128 MiB of HBM per device.

```python
import jax
import jax.numpy as jnp
from jax import lax

D = 16384
HQ = 8
HD = 128
TOK_DEV = 128
SECTIONS = 4
SEQ = 1024
QW = 1280
N_OUTER = 2
N_INNER = 4


def draw_projected(key, part):
    shape = (SECTIONS, SEQ, QW)
    result = jax.random.truncated_normal(key, -6.0, 6.0, shape, jnp.float32)
    return result.astype(jnp.bfloat16)


def draw_positions(key, part):
    span_count = 2 * N_OUTER * N_INNER
    half_shard = TOK_DEV // 2
    order = jax.random.permutation(key, span_count).astype(jnp.int32)
    rows_index = jnp.arange(SEQ, dtype=jnp.int32)
    return (order[rows_index // half_shard] * half_shard + rows_index % half_shard).astype(jnp.int32)


def draw_residual(key, part):
    shape = (SECTIONS, SEQ, D)
    first, second = jax.random.split(key)
    column_scale = 10.0 ** (jnp.arange(D, dtype=jnp.float32) / D)
    row_scale = 10.0 ** jax.random.uniform(second, (SECTIONS, SEQ, 1), jnp.float32, 0.0, 1.0)
    noise = jax.random.truncated_normal(first, -6.0, 6.0, shape, jnp.float32)
    return (0.012 * noise * row_scale * column_scale[None, None, :]).astype(jnp.bfloat16)


def block_scale(own_key, dims, pieces, low, high):
    level = 1.0
    for position, blocks in pieces:
        heights = jax.random.uniform(jax.random.fold_in(jax.random.fold_in(own_key, 6), position), (blocks,), jnp.float32, low / len(pieces), high / len(pieces))
        level = level * jnp.repeat(jnp.exp(heights), dims[position] // blocks).reshape((-1,) + (1,) * (len(dims) - 1 - position))
    return level


def gaussian(own_key, shape, width, bound, cuts=(), kind=jnp.bfloat16):
    drawn = jax.random.normal(own_key, shape, jnp.float32) * width
    if len(cuts) > 0:
        drawn = block_scale(own_key, shape, cuts, -0.22, 0.18) * drawn
    return jnp.clip(drawn, min=-bound, max=bound).astype(kind)


def setup_inputs(seed: int = 0) -> dict:
    splits = jax.random.split(jax.random.key(seed), 7)
    projected = draw_projected(jax.random.fold_in(splits[6], 71), 0)
    positions = draw_positions(jax.random.fold_in(splits[6], 71), 0)
    out_weight = gaussian(splits[2], (SECTIONS, HQ * HD, D), (3.0 / (HQ * HD) ** 0.5), 1.5, ((0, 4), (2, 8)))
    residual = draw_residual(jax.random.fold_in(splits[6], 71), 0)
    norm_gain = jnp.clip(1.0 + 0.18 * jax.random.normal(splits[4], (SECTIONS, D), jnp.float32), 0.099609375, 1.8984375).astype(jnp.bfloat16)
    next_weight = gaussian(splits[5], (SECTIONS, D, QW), D ** -0.5, 0.046875, ((0, 4), (1, 8)))
    return {"projected": projected, "positions": positions, "out_weight": out_weight, "residual": residual, "norm_gain": norm_gain, "next_weight": next_weight}


def attend_block(query_block, block_positions, keys, values, positions):
    scores = jnp.einsum('thd,jd->htj', query_block.astype(jnp.float32), keys.astype(jnp.float32)) * HD ** (-0.5)
    visible = positions[None, None, :] <= block_positions[None, :, None]
    scores = jnp.where(visible, scores, -jnp.inf)
    largest = lax.optimization_barrier(jnp.max(scores, axis=-1, keepdims=True))
    weights = jnp.where(visible, jnp.exp(scores - largest), 0.0)
    totals = lax.optimization_barrier(jnp.sum(weights, axis=-1))
    rounded = lax.optimization_barrier(weights.astype(jnp.bfloat16)).astype(jnp.float32)
    mixed = jnp.einsum('htj,jd->htd', rounded, values.astype(jnp.float32)) / totals[..., None]
    return jnp.transpose(mixed, (1, 0, 2)).reshape(-1, HQ * HD).astype(jnp.bfloat16)

def reference(projected, positions, out_weight, residual, norm_gain, next_weight):
    shard_count = N_OUTER * N_INNER

    def section_out(inputs):
        token_rows, weight_out, residual_rows = inputs
        queries = token_rows[:, :HQ * HD].reshape(shard_count, TOK_DEV, HQ, HD)
        keys = token_rows[:, HQ * HD:HQ * HD + HD]
        values = token_rows[:, HQ * HD + HD:]
        block_positions = positions.reshape(shard_count, TOK_DEV)
        attended = lax.map(lambda pair: attend_block(pair[0], pair[1], keys, values, positions), (queries, block_positions))
        attended = attended.reshape(SEQ, HQ * HD)
        product = jnp.dot(attended, weight_out, preferred_element_type=jnp.float32)
        return (residual_rows.astype(jnp.float32) + product).astype(jnp.bfloat16)
    hidden = lax.map(section_out, (projected, out_weight, residual))
    stream = jnp.roll(hidden, 1, axis=0)
    block_width = D // shard_count

    def section_in(inputs):
        stream_rows, gain, weight_next = inputs
        values32 = stream_rows.astype(jnp.float32)
        inverse_rms = lax.rsqrt(lax.optimization_barrier(jnp.mean(values32 * values32, axis=1)) + 1e-05)
        normed = (values32 * inverse_rms[:, None] * gain.astype(jnp.float32)[None, :]).astype(jnp.bfloat16)
        normed_blocks = jnp.transpose(normed.reshape(SEQ, shard_count, block_width), (1, 0, 2))
        weight_blocks = weight_next.reshape(shard_count, block_width, QW)

        def add_block(total, block_pair):
            partial_sum = jnp.dot(block_pair[0], block_pair[1], preferred_element_type=jnp.float32)
            partial_sum = lax.optimization_barrier(partial_sum.astype(jnp.bfloat16)).astype(jnp.float32)
            return (total + partial_sum, None)
        total, unused = lax.scan(add_block, jnp.zeros((SEQ, QW), jnp.float32), (normed_blocks, weight_blocks))
        return total.astype(jnp.bfloat16)
    next_projected = lax.map(section_in, (stream, norm_gain, next_weight))
    return (next_projected, stream)
```

```python
import functools

import jax
import jax.numpy as jnp
from jax import lax
from jax.experimental import pallas as pl
from jax.experimental.pallas import tpu as pltpu
from jax.sharding import PartitionSpec as P

HD = 128
LANES = 128
MESH = pl.DeviceIdType.MESH


def kernel(
    sizes,
    proj_ref,
    pos_ref,
    w1_hbm,
    res_hbm,
    gain_ref,
    w2_hbm,
    out_ref,
    stream_hbm,
    w1,
    res,
    w2,
    kv,
    att,
    hid,
    st,
    part,
    from_outer,
    from_inner,
    load_sem,
    store_sem,
    kv_inner_send,
    kv_outer_send,
    kv_recv,
    att_inner_send,
    att_outer_send,
    att_recv,
    hid_send,
    st_recv,
    px_send,
    px_recv,
    pz_send,
    pz_recv,
):
    sections, outers, inners, width = sizes
    shards = outers * inners
    sec = lax.axis_index("section")
    out = lax.axis_index("outer")
    inn = lax.axis_index("inner")
    me = out * inners + inn
    rows = proj_ref.shape[1]
    qw = proj_ref.shape[2]
    heads = (qw - 2 * HD) // HD
    cols = w1.shape[1]

    def shard_of(a, b):
        return lax.rem(out + a, outers) * inners + lax.rem(inn + b, inners)

    def outer_peer(a):
        return (sec, lax.rem(out + a, outers), inn)

    def inner_peer(b):
        return (sec, out, lax.rem(inn + b, inners))

    behind = (lax.rem(sec + sections - 1, sections), out, inn)
    ahead = (lax.rem(sec + 1, sections), out, inn)

    load_w1 = pltpu.make_async_copy(w1_hbm.at[0], w1, load_sem.at[0])
    load_res = pltpu.make_async_copy(res_hbm.at[0], res, load_sem.at[1])
    load_w2 = pltpu.make_async_copy(w2_hbm.at[0], w2, load_sem.at[2])
    load_w1.start()
    load_res.start()
    load_w2.start()

    barrier = pltpu.get_barrier_semaphore()
    peers = [outer_peer(a) for a in range(1, outers)]
    peers += [inner_peer(b) for b in range(1, inners)]
    peers += [behind, ahead]
    for peer in peers:
        pl.semaphore_signal(barrier, inc=1, device_id=peer, device_id_type=MESH)
    pl.semaphore_wait(barrier, len(peers))

    def remote(src, dst, send, recv, peer):
        return pltpu.make_async_remote_copy(
            src_ref=src,
            dst_ref=dst,
            send_sem=send,
            recv_sem=recv,
            device_id=peer,
            device_id_type=MESH,
        )

    def to_inner(buf, b, send, recv):
        return remote(buf.at[me], buf.at[me], send.at[b], recv.at[me], inner_peer(b))

    def to_outer(buf, a, b, send, recv):
        slot = shard_of(0, b)
        return remote(
            buf.at[slot], buf.at[slot], send.at[a, b], recv.at[slot], outer_peer(a)
        )

    def arrive(buf, slot, send, recv):
        remote(buf.at[slot], buf.at[slot], send.at[0], recv.at[slot], ahead).wait_recv()

    kv[me] = proj_ref[0, :, heads * HD :]
    for b in range(1, inners):
        to_inner(kv, b, kv_inner_send, kv_recv).start()
    for a in range(1, outers):
        to_outer(kv, a, 0, kv_outer_send, kv_recv).start()
    for b in range(1, inners):
        arrive(kv, shard_of(0, b), kv_inner_send, kv_recv)
        for a in range(1, outers):
            to_outer(kv, a, b, kv_outer_send, kv_recv).start()
    for b in range(inners):
        for a in range(1, outers):
            arrive(kv, shard_of(a, b), kv_inner_send, kv_recv)

    key_pos = pos_ref[...]
    own_pos = pos_ref[:, pl.ds(pl.multiple_of(me * rows, rows), rows)]
    own_col = jnp.transpose(
        jnp.broadcast_to(own_pos.astype(jnp.float32), (LANES, rows))
    )[:, :1]
    own_col = own_col.astype(jnp.int32)
    scale = HD ** (-0.5)

    def head_step(h, carry):
        at = pl.ds(pl.multiple_of(h * HD, HD), HD)
        queries = proj_ref[0, :, at]
        keys = kv[:, :, :HD].reshape(shards * rows, HD)
        values = kv[:, :, HD:].reshape(shards * rows, HD)
        scores = (
            lax.dot_general(
                queries, keys, (((1,), (1,)), ((), ())), preferred_element_type=jnp.float32
            )
            * scale
        )
        visible = key_pos <= own_col
        masked = jnp.where(visible, scores, -1e30)
        top = jnp.max(masked, axis=1, keepdims=True)
        weights = jnp.where(visible, jnp.exp(masked - top), 0.0)
        total = jnp.sum(weights, axis=1, keepdims=True)
        mixed = jnp.dot(weights.astype(jnp.bfloat16), values, preferred_element_type=jnp.float32)
        att[me, :, at] = (mixed / total).astype(jnp.bfloat16)
        return carry

    lax.fori_loop(0, heads, head_step, 0)

    for b in range(1, inners):
        to_inner(att, b, att_inner_send, att_recv).start()
    for a in range(1, outers):
        to_outer(att, a, 0, att_outer_send, att_recv).start()
    load_w1.wait()
    load_res.wait()
    load_w2.wait()

    def place(k):
        middle = k <= (inners - 1) * outers
        a = jnp.where(
            k == 0, 0, jnp.where(middle, lax.rem(k + outers - 1, outers), k - (inners - 1) * outers)
        )
        b = jnp.where(k == 0, 0, jnp.where(middle, (k + outers - 1) // outers, 0))
        return a, b

    def shift(slot):
        return remote(hid.at[slot], st.at[slot], hid_send.at[slot], st_recv.at[slot], ahead)

    def store(slot):
        at = pl.ds(pl.multiple_of(slot * rows, rows), rows)
        return pltpu.make_async_copy(st.at[slot], stream_hbm.at[0, at, :], store_sem.at[slot])

    def exchange(a, b):
        return remote(
            part.at[shard_of(a, b)],
            from_outer.at[a, b],
            px_send.at[a, b],
            px_recv.at[a, b],
            outer_peer(a),
        )

    def scatter(b):
        return remote(
            part.at[shard_of(0, b)], from_inner.at[b], pz_send.at[b], pz_recv.at[b], inner_peer(b)
        )

    def first(k):
        a, b = place(k)
        slot = shard_of(a, b)

        @pl.when(k > 0)
        def _():
            arrive(att, slot, att_inner_send, att_recv)

            @pl.when(a == 0)
            def _():
                for c in range(1, outers):
                    to_outer(att, c, b, att_outer_send, att_recv).start()

        at = pl.ds(pl.multiple_of(slot * rows, rows), rows)
        product = jnp.dot(att[slot], w1[...], preferred_element_type=jnp.float32)
        hid[slot] = (res[at, :].astype(jnp.float32) + product).astype(jnp.bfloat16)
        shift(slot).start()

    def second(k):
        a, b = place(k)
        slot = shard_of(a, b)
        shift(slot).wait_recv()
        store(slot).start()
        values = st[slot].astype(jnp.float32)
        scaled = (values * gain_ref[...].astype(jnp.float32)).astype(jnp.bfloat16)
        part[slot, :, :qw] = jnp.dot(
            scaled, w2[...], preferred_element_type=jnp.float32
        ).astype(jnp.bfloat16)
        squares = values * values
        lanes = squares[:, :LANES]
        for j in range(1, cols // LANES):
            lanes += squares[:, j * LANES : (j + 1) * LANES]
        part[slot, :, qw:] = lanes.astype(jnp.bfloat16)

        @pl.when(a > 0)
        def _():
            exchange(a, b).start()

    def combine(b):
        slot = shard_of(0, b)
        total = part[slot].astype(jnp.float32)
        for a in range(1, outers):
            exchange(a, b).wait_recv()
            total += from_outer[a, b].astype(jnp.float32)
        part[slot] = total.astype(jnp.bfloat16)
        scatter(b).start()

    lag = max(1, shards // 2)

    def step(k, carry):
        @pl.when(k < shards)
        def _():
            first(k)

        @pl.when(k >= lag)
        def _():
            second(k - lag)

            for b in range(1, inners):

                @pl.when(k - lag == min((b + 1) * outers, shards - 1))
                def _():
                    combine(b)

        return carry

    lax.fori_loop(0, shards + lag, step, 0)

    total = part[me].astype(jnp.float32)
    for a in range(1, outers):
        exchange(a, 0).wait_recv()
        total += from_outer[a, 0].astype(jnp.float32)
    for b in range(1, inners):
        scatter(b).wait_recv()
        total += from_inner[b].astype(jnp.float32)
    mean = jnp.sum(total[:, qw:], axis=1, keepdims=True) / width
    out_ref[0] = (total[:, :qw] * lax.rsqrt(mean + 1e-05)).astype(jnp.bfloat16)

    for b in range(1, inners):
        to_inner(kv, b, kv_inner_send, kv_recv).wait_send()
        to_inner(att, b, att_inner_send, att_recv).wait_send()
        scatter(b).wait_send()
    for a in range(1, outers):
        for b in range(inners):
            to_outer(kv, a, b, kv_outer_send, kv_recv).wait_send()
            to_outer(att, a, b, att_outer_send, att_recv).wait_send()
            exchange(a, b).wait_send()

    def drain(slot, carry):
        shift(slot).wait_send()
        store(slot).wait()
        return carry

    lax.fori_loop(0, shards, drain, 0)


def body(mesh, projected, positions, out_weight, residual, norm_gain, next_weight):
    sections, outers, inners = (mesh.shape[n] for n in ("section", "outer", "inner"))
    shards = outers * inners
    rows, qw = projected.shape[1:]
    inner_width, cols = out_weight.shape[1:]
    seq = positions.shape[0]
    wide = qw + LANES
    bf16 = jnp.bfloat16
    dma = pltpu.SemaphoreType.DMA
    vmem = pl.BlockSpec(memory_space=pltpu.VMEM)
    hbm = pl.BlockSpec(memory_space=pl.ANY)
    return pl.pallas_call(
        functools.partial(kernel, (sections, outers, inners, cols * shards)),
        out_shape=(
            jax.ShapeDtypeStruct((1, rows, qw), bf16),
            jax.ShapeDtypeStruct((1, seq, cols), bf16),
        ),
        in_specs=[vmem, vmem, hbm, hbm, vmem, hbm],
        out_specs=(vmem, hbm),
        scratch_shapes=[
            pltpu.VMEM((inner_width, cols), bf16),
            pltpu.VMEM((seq, cols), bf16),
            pltpu.VMEM((cols, qw), bf16),
            pltpu.VMEM((shards, rows, 2 * HD), bf16),
            pltpu.VMEM((shards, rows, inner_width), bf16),
            pltpu.VMEM((shards, rows, cols), bf16),
            pltpu.VMEM((shards, rows, cols), bf16),
            pltpu.VMEM((shards, rows, wide), bf16),
            pltpu.VMEM((outers, inners, rows, wide), bf16),
            pltpu.VMEM((inners, rows, wide), bf16),
            dma((3,)),
            dma((shards,)),
            dma((inners,)),
            dma((outers, inners)),
            dma((shards,)),
            dma((inners,)),
            dma((outers, inners)),
            dma((shards,)),
            dma((shards,)),
            dma((shards,)),
            dma((outers, inners)),
            dma((outers, inners)),
            dma((inners,)),
            dma((inners,)),
        ],
        compiler_params=pltpu.CompilerParams(
            collective_id=0, has_side_effects=True, vmem_limit_bytes=63 * 1024 * 1024
        ),
    )(
        projected,
        positions.reshape(1, seq),
        out_weight,
        residual,
        norm_gain.reshape(1, cols),
        next_weight,
    )


def solution(mesh):
    return jax.shard_map(
        functools.partial(body, mesh),
        mesh=mesh,
        in_specs=(
            P("section", ("outer", "inner"), None),
            P(),
            P("section", None, ("outer", "inner")),
            P("section", None, ("outer", "inner")),
            P("section", ("outer", "inner")),
            P("section", ("outer", "inner"), None),
        ),
        out_specs=(P("section", ("outer", "inner"), None), P("section", None, ("outer", "inner"))),
        check_vma=False,
    )
```

```python
import functools

import jax
import jax.numpy as jnp
from jax import lax
from jax.experimental import pallas as pl
from jax.experimental.pallas import tpu as pltpu
from jax.sharding import PartitionSpec as P

HD = 128
LANES = 128
MESH = pl.DeviceIdType.MESH


def kernel(
    sizes,
    proj_ref,
    pos_ref,
    w1_hbm,
    res_hbm,
    gain_ref,
    w2_hbm,
    out_ref,
    stream_hbm,
    w1,
    res,
    w2,
    kv,
    att,
    hid,
    st,
    part,
    from_outer,
    from_inner,
    load_sem,
    store_sem,
    kv_inner_send,
    kv_outer_send,
    kv_recv,
    att_inner_send,
    att_outer_send,
    att_recv,
    hid_send,
    st_recv,
    px_send,
    px_recv,
    pz_send,
    pz_recv,
):
    sections, outers, inners, width = sizes
    shards = outers * inners
    sec = lax.axis_index("section")
    out = lax.axis_index("outer")
    inn = lax.axis_index("inner")
    me = out * inners + inn
    rows = proj_ref.shape[1]
    qw = proj_ref.shape[2]
    heads = (qw - 2 * HD) // HD
    cols = w1.shape[1]

    last = inners - 1
    near = jnp.minimum(inn, last - inn)

    def nearest(t):
        paired = jnp.where(lax.rem(t, 2) == 1, inn - (t + 1) // 2, inn + (t + 1) // 2)
        single = jnp.where(inn == near, inn + t - near, inn - t + near)
        return jnp.where(t <= 2 * near, paired, single)

    def shard_of(a, t):
        return lax.rem(out + a, outers) * inners + nearest(t)

    def outer_peer(a):
        return (sec, lax.rem(out + a, outers), inn)

    def inner_peer(b):
        return (sec, out, lax.rem(inn + b, inners))

    behind = (lax.rem(sec + sections - 1, sections), out, inn)
    ahead = (lax.rem(sec + 1, sections), out, inn)

    load_w1 = pltpu.make_async_copy(w1_hbm.at[0], w1, load_sem.at[0])
    load_res = pltpu.make_async_copy(res_hbm.at[0], res, load_sem.at[1])
    load_w2 = pltpu.make_async_copy(w2_hbm.at[0], w2, load_sem.at[2])
    load_w1.start()
    load_res.start()
    load_w2.start()

    barrier = pltpu.get_barrier_semaphore()
    peers = [outer_peer(a) for a in range(1, outers)]
    peers += [inner_peer(b) for b in range(1, inners)]
    peers += [behind, ahead]
    for peer in peers:
        pl.semaphore_signal(barrier, inc=1, device_id=peer, device_id_type=MESH)
    pl.semaphore_wait(barrier, len(peers))

    def remote(src, dst, send, recv, peer):
        return pltpu.make_async_remote_copy(
            src_ref=src,
            dst_ref=dst,
            send_sem=send,
            recv_sem=recv,
            device_id=peer,
            device_id_type=MESH,
        )

    def along(buf, t, send, recv, up):
        slot = shard_of(0, t)
        peer = (sec, out, inn + 1 if up else inn - 1)
        return remote(buf.at[slot], buf.at[slot], send.at[int(up), t], recv.at[slot], peer)

    def relay(buf, t, send, recv, done=False):
        origin = nearest(t)

        @pl.when(jnp.logical_and(origin <= inn, inn < last))
        def _():
            copy = along(buf, t, send, recv, True)
            copy.wait_send() if done else copy.start()

        @pl.when(jnp.logical_and(origin >= inn, inn > 0))
        def _():
            copy = along(buf, t, send, recv, False)
            copy.wait_send() if done else copy.start()

    def to_outer(buf, a, b, send, recv):
        slot = shard_of(0, b)
        return remote(
            buf.at[slot], buf.at[slot], send.at[a, b], recv.at[slot], outer_peer(a)
        )

    def arrive(buf, slot, send, recv):
        remote(buf.at[slot], buf.at[slot], send.at[0, 0], recv.at[slot], ahead).wait_recv()

    kv[me] = proj_ref[0, :, heads * HD :]
    relay(kv, 0, kv_inner_send, kv_recv)
    for a in range(1, outers):
        to_outer(kv, a, 0, kv_outer_send, kv_recv).start()
    for b in range(1, inners):
        arrive(kv, shard_of(0, b), kv_inner_send, kv_recv)
        relay(kv, b, kv_inner_send, kv_recv)
        for a in range(1, outers):
            to_outer(kv, a, b, kv_outer_send, kv_recv).start()
    for b in range(inners):
        for a in range(1, outers):
            arrive(kv, shard_of(a, b), kv_inner_send, kv_recv)

    key_pos = pos_ref[...]
    own_pos = pos_ref[:, pl.ds(pl.multiple_of(me * rows, rows), rows)]
    own_col = jnp.transpose(
        jnp.broadcast_to(own_pos.astype(jnp.float32), (LANES, rows))
    )[:, :1]
    own_col = own_col.astype(jnp.int32)
    scale = HD ** (-0.5)

    def head_step(h, carry):
        at = pl.ds(pl.multiple_of(h * HD, HD), HD)
        queries = proj_ref[0, :, at]
        keys = kv[:, :, :HD].reshape(shards * rows, HD)
        values = kv[:, :, HD:].reshape(shards * rows, HD)
        scores = (
            lax.dot_general(
                queries, keys, (((1,), (1,)), ((), ())), preferred_element_type=jnp.float32
            )
            * scale
        )
        visible = key_pos <= own_col
        masked = jnp.where(visible, scores, -1e30)
        top = jnp.max(masked, axis=1, keepdims=True)
        weights = jnp.where(visible, jnp.exp(masked - top), 0.0)
        total = jnp.sum(weights, axis=1, keepdims=True)
        mixed = jnp.dot(weights.astype(jnp.bfloat16), values, preferred_element_type=jnp.float32)
        att[me, :, at] = (mixed / total).astype(jnp.bfloat16)
        return carry

    lax.fori_loop(0, heads, head_step, 0)

    relay(att, 0, att_inner_send, att_recv)
    for a in range(1, outers):
        to_outer(att, a, 0, att_outer_send, att_recv).start()
    load_w1.wait()
    load_res.wait()
    load_w2.wait()

    tail = 2 + (inners - 2) * outers

    def place(k):
        turn, rank = lax.rem(k + 2 * outers - 2, outers), 2 + (k - 2) // outers
        left = k - tail
        a = jnp.where(k < tail, turn, jnp.where(left < outers - 1, 1 + left, 2 + left - outers))
        t = jnp.where(
            k < tail,
            jnp.where(turn == 0, rank, rank - 1),
            jnp.where(left < outers - 1, inners - 1, 0),
        )
        return jnp.where(k < 2, 0, a), jnp.where(k < 2, k, t)

    def shift(slot):
        return remote(hid.at[slot], st.at[slot], hid_send.at[slot], st_recv.at[slot], ahead)

    def store(slot):
        at = pl.ds(pl.multiple_of(slot * rows, rows), rows)
        return pltpu.make_async_copy(st.at[slot], stream_hbm.at[0, at, :], store_sem.at[slot])

    def exchange(a, b):
        return remote(
            part.at[shard_of(a, b)],
            from_outer.at[a, b],
            px_send.at[a, b],
            px_recv.at[a, b],
            outer_peer(a),
        )

    def scatter(b):
        return remote(
            part.at[shard_of(0, b)],
            from_inner.at[inn],
            pz_send.at[b],
            pz_recv.at[inn],
            (sec, out, nearest(b)),
        )

    def gathered(b):
        peer = nearest(b)
        return remote(part.at[me], from_inner.at[peer], pz_send.at[0], pz_recv.at[peer], ahead)

    def first(k):
        a, b = place(k)
        slot = shard_of(a, b)

        @pl.when(k > 0)
        def _():
            arrive(att, slot, att_inner_send, att_recv)

            @pl.when(a == 0)
            def _():
                relay(att, b, att_inner_send, att_recv)
                for c in range(1, outers):
                    to_outer(att, c, b, att_outer_send, att_recv).start()

        at = pl.ds(pl.multiple_of(slot * rows, rows), rows)
        product = jnp.dot(att[slot], w1[...], preferred_element_type=jnp.float32)
        hid[slot] = (res[at, :].astype(jnp.float32) + product).astype(jnp.bfloat16)
        shift(slot).start()

    def second(k):
        a, b = place(k)
        slot = shard_of(a, b)
        shift(slot).wait_recv()
        store(slot).start()
        values = st[slot].astype(jnp.float32)
        scaled = (values * gain_ref[...].astype(jnp.float32)).astype(jnp.bfloat16)
        part[slot, :, :qw] = jnp.dot(
            scaled, w2[...], preferred_element_type=jnp.float32
        ).astype(jnp.bfloat16)
        squares = values * values
        lanes = squares[:, :LANES]
        for j in range(1, cols // LANES):
            lanes += squares[:, j * LANES : (j + 1) * LANES]
        part[slot, :, qw:] = lanes.astype(jnp.bfloat16)

        @pl.when(a > 0)
        def _():
            exchange(a, b).start()

    def combine(b):
        slot = shard_of(0, b)
        total = part[slot].astype(jnp.float32)
        for a in range(1, outers):
            exchange(a, b).wait_recv()
            total += from_outer[a, b].astype(jnp.float32)
        part[slot] = total.astype(jnp.bfloat16)
        scatter(b).start()

    lag = max(1, 3 * shards // 8)

    def step(k, carry):
        @pl.when(k < shards)
        def _():
            first(k)

        @pl.when(k >= lag)
        def _():
            second(k - lag)

            for b in range(1, inners):

                @pl.when(k - lag == min(2 + b * outers, tail + outers - 1))
                def _():
                    combine(b)

        return carry

    lax.fori_loop(0, shards + lag, step, 0)

    total = part[me].astype(jnp.float32)
    for a in range(1, outers):
        exchange(a, 0).wait_recv()
        total += from_outer[a, 0].astype(jnp.float32)
    for b in range(1, inners):
        gathered(b).wait_recv()
        total += from_inner[nearest(b)].astype(jnp.float32)
    mean = jnp.sum(total[:, qw:], axis=1, keepdims=True) / width
    out_ref[0] = (total[:, :qw] * lax.rsqrt(mean + 1e-05)).astype(jnp.bfloat16)

    for b in range(1, inners):
        scatter(b).wait_send()
    for a in range(1, outers):
        for b in range(inners):
            to_outer(kv, a, b, kv_outer_send, kv_recv).wait_send()
            to_outer(att, a, b, att_outer_send, att_recv).wait_send()
            exchange(a, b).wait_send()

    for b in range(inners):
        relay(kv, b, kv_inner_send, kv_recv, True)
        relay(att, b, att_inner_send, att_recv, True)

    def drain(slot, carry):
        shift(slot).wait_send()
        store(slot).wait()
        return carry

    lax.fori_loop(0, shards, drain, 0)


def body(mesh, projected, positions, out_weight, residual, norm_gain, next_weight):
    sections, outers, inners = (mesh.shape[n] for n in ("section", "outer", "inner"))
    shards = outers * inners
    rows, qw = projected.shape[1:]
    inner_width, cols = out_weight.shape[1:]
    seq = positions.shape[0]
    wide = qw + LANES
    bf16 = jnp.bfloat16
    dma = pltpu.SemaphoreType.DMA
    vmem = pl.BlockSpec(memory_space=pltpu.VMEM)
    hbm = pl.BlockSpec(memory_space=pl.ANY)
    return pl.pallas_call(
        functools.partial(kernel, (sections, outers, inners, cols * shards)),
        out_shape=(
            jax.ShapeDtypeStruct((1, rows, qw), bf16),
            jax.ShapeDtypeStruct((1, seq, cols), bf16),
        ),
        in_specs=[vmem, vmem, hbm, hbm, vmem, hbm],
        out_specs=(vmem, hbm),
        scratch_shapes=[
            pltpu.VMEM((inner_width, cols), bf16),
            pltpu.VMEM((seq, cols), bf16),
            pltpu.VMEM((cols, qw), bf16),
            pltpu.VMEM((shards, rows, 2 * HD), bf16),
            pltpu.VMEM((shards, rows, inner_width), bf16),
            pltpu.VMEM((shards, rows, cols), bf16),
            pltpu.VMEM((shards, rows, cols), bf16),
            pltpu.VMEM((shards, rows, wide), bf16),
            pltpu.VMEM((outers, inners, rows, wide), bf16),
            pltpu.VMEM((inners, rows, wide), bf16),
            dma((3,)),
            dma((shards,)),
            dma((2, inners)),
            dma((outers, inners)),
            dma((shards,)),
            dma((2, inners)),
            dma((outers, inners)),
            dma((shards,)),
            dma((shards,)),
            dma((shards,)),
            dma((outers, inners)),
            dma((outers, inners)),
            dma((inners,)),
            dma((inners,)),
        ],
        compiler_params=pltpu.CompilerParams(
            collective_id=0, has_side_effects=True, vmem_limit_bytes=63 * 1024 * 1024
        ),
    )(
        projected,
        positions.reshape(1, seq),
        out_weight,
        residual,
        norm_gain.reshape(1, cols),
        next_weight,
    )


def solution(mesh):
    return jax.shard_map(
        functools.partial(body, mesh),
        mesh=mesh,
        in_specs=(
            P("section", ("outer", "inner"), None),
            P(),
            P("section", None, ("outer", "inner")),
            P("section", None, ("outer", "inner")),
            P("section", ("outer", "inner")),
            P("section", ("outer", "inner"), None),
        ),
        out_specs=(P("section", ("outer", "inner"), None), P("section", None, ("outer", "inner"))),
        check_vma=False,
    )
```

```python
import functools
import math

import jax
import jax.numpy as jnp
from jax import lax
from jax.experimental import pallas as pl
from jax.experimental.pallas import tpu as pltpu
from jax.sharding import PartitionSpec as P

HD = 128
LANES = 128
MESH = pl.DeviceIdType.MESH


def kernel(
    sizes,
    proj_ref,
    pos_ref,
    w1_hbm,
    res_hbm,
    gain_ref,
    w2_hbm,
    out_ref,
    stream_hbm,
    w1,
    res,
    w2,
    kv,
    att,
    hid,
    st,
    part,
    from_outer,
    from_inner,
    load_sem,
    store_sem,
    kv_inner_send,
    kv_outer_send,
    kv_recv,
    att_inner_send,
    att_outer_send,
    att_recv,
    hid_send,
    st_recv,
    px_send,
    px_recv,
    pz_send,
    pz_recv,
):
    sections, outers, inners, width = sizes
    shards = outers * inners
    sec = lax.axis_index("section")
    out = lax.axis_index("outer")
    inn = lax.axis_index("inner")
    me = out * inners + inn
    rows = proj_ref.shape[1]
    qw = proj_ref.shape[2]
    heads = (qw - 2 * HD) // HD
    cols = w1.shape[1]

    last = inners - 1
    near = jnp.minimum(inn, last - inn)

    def nearest(t):
        paired = jnp.where(lax.rem(t, 2) == 1, inn - (t + 1) // 2, inn + (t + 1) // 2)
        single = jnp.where(inn == near, inn + t - near, inn - t + near)
        return jnp.where(t <= 2 * near, paired, single)

    def shard_of(a, t):
        return lax.rem(out + a, outers) * inners + nearest(t)

    def outer_peer(a):
        return (sec, lax.rem(out + a, outers), inn)

    def inner_peer(b):
        return (sec, out, lax.rem(inn + b, inners))

    behind = (lax.rem(sec + sections - 1, sections), out, inn)
    ahead = (lax.rem(sec + 1, sections), out, inn)

    load_w1 = pltpu.make_async_copy(w1_hbm.at[0], w1, load_sem.at[0])
    load_res = pltpu.make_async_copy(res_hbm.at[0], res, load_sem.at[1])
    load_w2 = pltpu.make_async_copy(w2_hbm.at[0], w2, load_sem.at[2])
    load_w1.start()
    load_res.start()
    load_w2.start()

    barrier = pltpu.get_barrier_semaphore()
    peers = [outer_peer(a) for a in range(1, outers)]
    peers += [inner_peer(b) for b in range(1, inners)]
    peers += [behind, ahead]
    for peer in peers:
        pl.semaphore_signal(barrier, inc=1, device_id=peer, device_id_type=MESH)
    pl.semaphore_wait(barrier, len(peers))

    def remote(src, dst, send, recv, peer):
        return pltpu.make_async_remote_copy(
            src_ref=src,
            dst_ref=dst,
            send_sem=send,
            recv_sem=recv,
            device_id=peer,
            device_id_type=MESH,
        )

    def along(buf, t, send, recv, up):
        slot = shard_of(0, t)
        peer = (sec, out, inn + 1 if up else inn - 1)
        return remote(buf.at[slot], buf.at[slot], send.at[int(up), t], recv.at[slot], peer)

    def relay(buf, t, send, recv, done=False):
        origin = nearest(t)

        @pl.when(jnp.logical_and(origin <= inn, inn < last))
        def _():
            copy = along(buf, t, send, recv, True)
            copy.wait_send() if done else copy.start()

        @pl.when(jnp.logical_and(origin >= inn, inn > 0))
        def _():
            copy = along(buf, t, send, recv, False)
            copy.wait_send() if done else copy.start()

    def to_outer(buf, a, b, send, recv):
        slot = shard_of(0, b)
        return remote(
            buf.at[slot], buf.at[slot], send.at[a, b], recv.at[slot], outer_peer(a)
        )

    def arrive(buf, slot, send, recv):
        remote(buf.at[slot], buf.at[slot], send.at[0, 0], recv.at[slot], ahead).wait_recv()

    kv[me] = proj_ref[0, :, heads * HD :]
    relay(kv, 0, kv_inner_send, kv_recv)
    for a in range(1, outers):
        to_outer(kv, a, 0, kv_outer_send, kv_recv).start()
    for b in range(1, inners):
        arrive(kv, shard_of(0, b), kv_inner_send, kv_recv)
        relay(kv, b, kv_inner_send, kv_recv)
        for a in range(1, outers):
            to_outer(kv, a, b, kv_outer_send, kv_recv).start()
    for b in range(inners):
        for a in range(1, outers):
            arrive(kv, shard_of(a, b), kv_inner_send, kv_recv)

    key_pos = pos_ref[...]
    own_pos = pos_ref[:, pl.ds(pl.multiple_of(me * rows, rows), rows)]
    own_col = jnp.transpose(
        jnp.broadcast_to(own_pos.astype(jnp.float32), (LANES, rows))
    )[:, :1]
    own_col = own_col.astype(jnp.int32)
    scale = HD ** (-0.5)

    def head_step(h, carry):
        at = pl.ds(pl.multiple_of(h * HD, HD), HD)
        queries = proj_ref[0, :, at]
        keys = kv[:, :, :HD].reshape(shards * rows, HD)
        values = kv[:, :, HD:].reshape(shards * rows, HD)
        scores = (
            lax.dot_general(
                queries, keys, (((1,), (1,)), ((), ())), preferred_element_type=jnp.float32
            )
            * scale
        )
        visible = key_pos <= own_col
        masked = jnp.where(visible, scores, -1e30)
        top = jnp.max(masked, axis=1, keepdims=True)
        weights = jnp.where(visible, jnp.exp(masked - top), 0.0)
        total = jnp.sum(weights, axis=1, keepdims=True)
        mixed = jnp.dot(weights.astype(jnp.bfloat16), values, preferred_element_type=jnp.float32)
        att[me, :, at] = (mixed / total).astype(jnp.bfloat16)
        return carry

    lax.fori_loop(0, heads, head_step, 0)

    relay(att, 0, att_inner_send, att_recv)
    for a in range(1, outers):
        to_outer(att, a, 0, att_outer_send, att_recv).start()
    load_w1.wait()
    load_res.wait()
    load_w2.wait()

    others = outers - 1

    def place(k):
        beyond = jnp.maximum(k - inners, 0)
        block = beyond // others
        t = jnp.where(block < inners - 2, 2 + block, inners - 1 - block)
        inside = k < inners
        return jnp.where(inside, 0, 1 + lax.rem(beyond, others)), jnp.where(inside, k, t)

    def ready(t):
        block = t - 2 if t > 1 else inners - 2
        return inners + (block + 2) * others - 1

    def shift(slot):
        return remote(hid.at[slot], st.at[slot], hid_send.at[slot], st_recv.at[slot], ahead)

    def store(slot):
        at = pl.ds(pl.multiple_of(slot * rows, rows), rows)
        return pltpu.make_async_copy(st.at[slot], stream_hbm.at[0, at, :], store_sem.at[slot])

    def exchange(a, b):
        return remote(
            part.at[shard_of(a, b)],
            from_outer.at[a, b],
            px_send.at[a, b],
            px_recv.at[a, b],
            outer_peer(a),
        )

    def scatter(b):
        return remote(
            part.at[shard_of(0, b)],
            from_inner.at[inn],
            pz_send.at[b],
            pz_recv.at[inn],
            (sec, out, nearest(b)),
        )

    def gathered(b):
        peer = nearest(b)
        return remote(part.at[me], from_inner.at[peer], pz_send.at[0], pz_recv.at[peer], ahead)

    def first(k):
        a, b = place(k)
        slot = shard_of(a, b)

        @pl.when(k > 0)
        def _():
            arrive(att, slot, att_inner_send, att_recv)

            @pl.when(a == 0)
            def _():
                relay(att, b, att_inner_send, att_recv)
                for c in range(1, outers):
                    to_outer(att, c, b, att_outer_send, att_recv).start()

        at = pl.ds(pl.multiple_of(slot * rows, rows), rows)
        product = jnp.dot(att[slot], w1[...], preferred_element_type=jnp.float32)
        hid[slot] = (res[at, :].astype(jnp.float32) + product).astype(jnp.bfloat16)
        shift(slot).start()

    def second(k):
        a, b = place(k)
        slot = shard_of(a, b)
        shift(slot).wait_recv()
        store(slot).start()
        values = st[slot].astype(jnp.float32)
        scaled = (values * gain_ref[...].astype(jnp.float32)).astype(jnp.bfloat16)
        part[slot, :, :qw] = jnp.dot(
            scaled, w2[...], preferred_element_type=jnp.float32
        ).astype(jnp.bfloat16)
        squares = values * values
        lanes = squares[:, :LANES]
        for j in range(1, cols // LANES):
            lanes += squares[:, j * LANES : (j + 1) * LANES]
        part[slot, :, qw:] = lanes.astype(jnp.bfloat16)

        @pl.when(a > 0)
        def _():
            exchange(a, b).start()

    def combine(b):
        slot = shard_of(0, b)
        total = part[slot].astype(jnp.float32)
        for a in range(1, outers):
            exchange(a, b).wait_recv()
            total += from_outer[a, b].astype(jnp.float32)
        part[slot] = total.astype(jnp.bfloat16)
        scatter(b).start()

    lag = max(1, shards // 4)

    def step(k, carry):
        @pl.when(k < shards)
        def _():
            first(k)

        @pl.when(k >= lag)
        def _():
            second(k - lag)

            for b in range(1, inners):

                @pl.when(k - lag == ready(b))
                def _():
                    combine(b)

        return carry

    lax.fori_loop(0, shards + lag, step, 0)

    total = part[me].astype(jnp.float32)
    for a in range(1, outers):
        exchange(a, 0).wait_recv()
        total += from_outer[a, 0].astype(jnp.float32)
    for b in range(1, inners):
        gathered(b).wait_recv()
        total += from_inner[nearest(b)].astype(jnp.float32)
    mean = jnp.sum(total[:, qw:], axis=1, keepdims=True) / width
    out_ref[0] = (total[:, :qw] * lax.rsqrt(mean + 1e-05)).astype(jnp.bfloat16)

    for b in range(1, inners):
        scatter(b).wait_send()
    for a in range(1, outers):
        for b in range(inners):
            to_outer(kv, a, b, kv_outer_send, kv_recv).wait_send()
            to_outer(att, a, b, att_outer_send, att_recv).wait_send()
            exchange(a, b).wait_send()

    for b in range(inners):
        relay(kv, b, kv_inner_send, kv_recv, True)
        relay(att, b, att_inner_send, att_recv, True)

    def drain(slot, carry):
        shift(slot).wait_send()
        store(slot).wait()
        return carry

    lax.fori_loop(0, shards, drain, 0)


def body(mesh, projected, positions, out_weight, residual, norm_gain, next_weight):
    sections, outers, inners = (mesh.shape[n] for n in ("section", "outer", "inner"))
    shards = outers * inners
    rows, qw = projected.shape[1:]
    inner_width, cols = out_weight.shape[1:]
    seq = positions.shape[0]
    wide = qw + LANES
    bf16 = jnp.bfloat16
    dma = pltpu.SemaphoreType.DMA
    vmem = pl.BlockSpec(memory_space=pltpu.VMEM)
    hbm = pl.BlockSpec(memory_space=pl.ANY)
    shapes = (
        (inner_width, cols),
        (seq, cols),
        (cols, qw),
        (shards, rows, 2 * HD),
        (shards, rows, inner_width),
        (shards, rows, cols),
        (shards, rows, cols),
        (shards, rows, wide),
        (outers, inners, rows, wide),
        (inners, rows, wide),
    )
    scratch = sum(2 * math.prod(shape) for shape in shapes)
    grant = min(63, scratch // 2**20 + 18) * 2**20
    return pl.pallas_call(
        functools.partial(kernel, (sections, outers, inners, cols * shards)),
        out_shape=(
            jax.ShapeDtypeStruct((1, rows, qw), bf16),
            jax.ShapeDtypeStruct((1, seq, cols), bf16),
        ),
        in_specs=[vmem, vmem, hbm, hbm, vmem, hbm],
        out_specs=(vmem, hbm),
        scratch_shapes=[
            *(pltpu.VMEM(shape, bf16) for shape in shapes),
            dma((3,)),
            dma((shards,)),
            dma((2, inners)),
            dma((outers, inners)),
            dma((shards,)),
            dma((2, inners)),
            dma((outers, inners)),
            dma((shards,)),
            dma((shards,)),
            dma((shards,)),
            dma((outers, inners)),
            dma((outers, inners)),
            dma((inners,)),
            dma((inners,)),
        ],
        compiler_params=pltpu.CompilerParams(
            collective_id=0, has_side_effects=True, vmem_limit_bytes=grant
        ),
    )(
        projected,
        positions.reshape(1, seq),
        out_weight,
        residual,
        norm_gain.reshape(1, cols),
        next_weight,
    )


def solution(mesh):
    return jax.shard_map(
        functools.partial(body, mesh),
        mesh=mesh,
        in_specs=(
            P("section", ("outer", "inner"), None),
            P(),
            P("section", None, ("outer", "inner")),
            P("section", None, ("outer", "inner")),
            P("section", ("outer", "inner")),
            P("section", ("outer", "inner"), None),
        ),
        out_specs=(P("section", ("outer", "inner"), None), P("section", None, ("outer", "inner"))),
        check_vma=False,
    )
```
